32 devices in a mesh: expert: 8 (over z, y), dp: 2 (over x), outer: 2 (over core).
Axes of the slice: x: 2, y: 2, z: 4, core: 2. Of those that a mesh axis runs over, the one named last changes fastest.
Arguments:
- tokens: bfloat16 [4096, 1024], P(('expert', 'dp', 'outer')), may hold values from -6 to 6
- cotangent: bfloat16 [4096, 1024], P(('expert', 'dp', 'outer')), may hold values from -6 to 6
- expert_ids: int32 [4096, 2], P(('expert', 'dp', 'outer')), may hold values from 0 to 7, all different within a row; in each aligned block of 128 rows (0 to 127, 128 to 255, ...) at most 40 rows name the same one
- route_prob: float32 [4096, 2], P(('expert', 'dp', 'outer')), may hold values from 0.1 to 1
- popularity: int32 [8], replicated, may hold values from 0 to 7, each once
- w_gate: bfloat16 [8, 704, 1024], P('expert'), may hold values from -0.1875 to 0.1875
- w_up: bfloat16 [8, 704, 1024], P('expert'), may hold values from -0.1875 to 0.1875
- w_down: bfloat16 [8, 704, 1024], P('expert'), may hold values from -0.21875 to 0.21875
Outputs:
- token_grad: bfloat16 [4096, 1024], P(('expert', 'dp', 'outer'))
- weight_grad: float32 [704, 8, 1024], P(('dp', 'outer'), 'expert')
The draws below stay inside these ranges and needn't reach their ends.
Inputs may be any that keep to these rules, and one draw needn't show every extreme that they name: `expert_ids`: each row names 2 different experts. Among the rows of one device no expert is named by more than 40 rows, and some device reaches 40 for some expert. `popularity`: each expert id appears once.
All inputs are finite; a program needn't handle non-finite values.
Results may differ from the reference program's by a relative error of at most 0.008.
Values may be sent and summed in bfloat16 or wider, within the bound.
A program may use at most 64 MiB of HBM per device.

```python
import math
import jax
import jax.numpy as jnp
import numpy as np
from jax import lax

D = 1024
F = 704
TOP = 2
TOK_DEV = 128
EXPERTS = 8
CAP = 40
TOKENS = 4096
N_EXPERT = 8
N_DP = 2
N_OUTER = 2


def shard_levels(stream_key, extent, split, smallest, largest):
    def one(position, parts):
        steps = jax.random.uniform(jax.random.fold_in(jax.random.fold_in(stream_key, 6), position), (parts,), jnp.float32, smallest / len(split), largest / len(split))
        return jnp.repeat(jnp.exp(steps), extent[position] // parts).reshape((-1,) + (1,) * (len(extent) - position - 1))

    loudness = one(*split[0])
    for cut in split[1:]:
        loudness = loudness * one(*cut)
    return loudness


def routed_block(own_key, own, number, rows, amount, top, limit, lean):
    order = jax.random.permutation(own_key, amount)
    heavy_load, common = load_shares(amount, rows * top, limit, lean, True), load_shares(amount, rows * top, limit, lean, False)
    places = jnp.arange(amount)

    def named(sizes, rotation):
        used = int((sizes > 0).sum())
        fixed = max(1, used // 4)
        shifted = fixed + (places - fixed + rotation * (used - fixed)) % max(1, amount - fixed)
        return jnp.zeros((amount,), jnp.int32).at[order[jnp.where(places < fixed, places, shifted)]].set(jnp.asarray(sizes, jnp.int32))

    sizes = jnp.where(number % 4 == 0, named(heavy_load, number // 4), named(common, number - number // 4 - 1))
    mixed = jax.random.permutation(jax.random.fold_in(own, 3), amount)
    donor, sink = mixed[0:amount // 2 * 2:2], mixed[1:amount // 2 * 2:2]
    margin = jnp.minimum(sizes[donor] - 1, limit - sizes[sink]) // 2
    margin = jnp.where((donor == order[0]) | (sink == order[0]) | (sizes[sink] == 0), 0, jnp.maximum(margin, 0))
    shifted = jax.random.randint(jax.random.fold_in(own, 4), (amount // 2,), 0, 1 << 20) % (margin + 1)
    sizes = sizes.at[donor].add(-shifted).at[sink].add(shifted)
    items = jnp.searchsorted(jnp.cumsum(sizes), jnp.arange(rows * top), side="right").astype(jnp.int32)
    listing = items.reshape(top, rows).T
    listing = listing[jax.random.permutation(jax.random.fold_in(own, 1), rows)]
    rotation = jax.random.randint(jax.random.fold_in(own, 2), (rows, 1), 0, top)
    return jnp.take_along_axis(listing, (jnp.arange(top)[None, :] + rotation) % top, axis=1)


def load_shares(count, total, reach, skew, full):
    loads = [(1 << 20) // math.isqrt(standing ** skew) + 1 for standing in range(1, count + 1)]
    largest = reach if full else min(reach, max(-(-total // count), total * loads[0] // sum(loads)))
    least = 1 if total - largest >= count - 1 else 0
    counts, rest = [largest] + [least] * (count - 1), total - largest - least * (count - 1)
    while rest > 0:
        free = [i for i in range(1, count) if counts[i] < largest] or [i for i in range(1, count) if counts[i] < reach]
        mass, budget = sum([loads[i] for i in free]), rest
        for i in free:
            extra = min(reach - counts[i], max(1, budget * loads[i] // mass), rest)
            counts[i] = counts[i] + extra
            rest = rest - extra
    return np.array(counts)


def gaussian(rng, dims, deviation, bound, split=(), kind=jnp.bfloat16):
    array = deviation * jax.random.normal(rng, dims, jnp.float32)
    if split:
        array = array * shard_levels(rng, dims, split, -0.22, 0.18)
    return jnp.clip(array, -bound, bound).astype(kind)


def setup_inputs(seed: int = 0) -> dict:
    arg_keys = jax.random.split(jax.random.key(seed), 9)
    tokens = gaussian(arg_keys[0], (TOKENS, D), 1.0, 6.0, ((0, 32),))
    cotangent = gaussian(arg_keys[1], (TOKENS, D), 1.0, 6.0, ((0, 32),))
    expert_ids_keys = jax.random.split(jax.random.fold_in(arg_keys[2], 1), TOKENS // TOK_DEV)
    expert_ids_turns = jax.random.permutation(jax.random.fold_in(arg_keys[2], 3), TOKENS // TOK_DEV)
    expert_ids = jax.vmap(lambda own, number: routed_block(jax.random.fold_in(arg_keys[2], 2), own, number, TOK_DEV, EXPERTS, TOP, CAP, 2))(expert_ids_keys, expert_ids_turns).reshape((TOKENS, TOP))
    route_prob = jnp.clip(0.1 + 0.9 * jax.random.uniform(arg_keys[3], (TOKENS, TOP), jnp.float32) ** shard_levels(arg_keys[3], (TOKENS, TOP), ((0, 32),), -0.2, 0.2), 0.1, 1.0)
    popularity = jax.random.permutation(arg_keys[4], EXPERTS).astype(jnp.int32)
    w_gate = gaussian(arg_keys[5], (EXPERTS, F, D), D ** -0.5, 0.1875, ((0, 8),))
    w_up = gaussian(arg_keys[6], (EXPERTS, F, D), D ** -0.5, 0.1875, ((0, 8),))
    w_down = gaussian(arg_keys[7], (EXPERTS, F, D), F ** -0.5, 0.21875, ((0, 8),))
    return {"tokens": tokens, "cotangent": cotangent, "expert_ids": expert_ids, "route_prob": route_prob, "popularity": popularity, "w_gate": w_gate, "w_up": w_up, "w_down": w_down}


def replica_sum(left_rows, right_rows, replicas):
    left_all = left_rows.astype(jnp.float32).reshape(replicas, -1, left_rows.shape[1])
    right_all = right_rows.astype(jnp.float32).reshape(replicas, -1, right_rows.shape[1])
    partials = jnp.einsum("rnf,rnd->rfd", left_all, right_all).astype(jnp.bfloat16)
    partials = lax.optimization_barrier(partials)
    return jnp.sum(partials.astype(jnp.float32), axis=0) * (1.0 / replicas)


def reference(tokens, cotangent, expert_ids, route_prob, popularity, w_gate, w_up, w_down):
    replicas = N_DP * N_OUTER
    device_count = N_EXPERT * replicas
    assigned = TOK_DEV * TOP
    onehot = (expert_ids[:, :, None] == popularity[None, None, :]).astype(jnp.int32)
    onehot = onehot.reshape(device_count, assigned, EXPERTS)
    before = jnp.cumsum(onehot, axis=1) - onehot
    place_rank = jnp.sum(onehot * before, axis=2)
    slot_index = jnp.sum(onehot * jnp.arange(EXPERTS, dtype=jnp.int32)[None, None, :], axis=2)
    device_index = jnp.arange(device_count, dtype=jnp.int32)[:, None]
    source = device_index // replicas
    replica = device_index % replicas
    target = (((slot_index * replicas + replica) * N_EXPERT + source) * CAP + place_rank).reshape(-1)
    token_index = (device_index * TOK_DEV + jnp.arange(assigned, dtype=jnp.int32)[None, :] // TOP).reshape(-1)
    slot_rows = replicas * N_EXPERT * CAP
    total_slots = EXPERTS * slot_rows
    token_table = jnp.full((total_slots,), -1, jnp.int32).at[target].set(token_index)
    token_table = token_table.reshape(EXPERTS, slot_rows)
    prob_table = jnp.zeros((total_slots,), jnp.float32).at[target].set(route_prob.reshape(-1).astype(jnp.float32))
    prob_table = prob_table.reshape(EXPERTS, slot_rows)

    def one_expert(running, inputs):
        table_row, prob_row, gate_mat, up_mat, down_mat = inputs
        is_live = table_row >= 0
        safe_index = jnp.maximum(table_row, 0)
        gathered = jnp.where(is_live[:, None], tokens[safe_index], jnp.zeros((), tokens.dtype))
        cot_rows = (prob_row[:, None] * cotangent[safe_index].astype(jnp.float32)).astype(jnp.bfloat16)
        gate_pre = jnp.dot(gathered, gate_mat.T, preferred_element_type=jnp.float32)
        up_proj = jnp.dot(gathered, up_mat.T, preferred_element_type=jnp.float32)
        hidden_grad = jnp.dot(cot_rows, down_mat.T, preferred_element_type=jnp.float32)
        sigmoid_gate = jax.nn.sigmoid(gate_pre)
        hidden = (gate_pre * sigmoid_gate * up_proj).astype(jnp.bfloat16)
        gate_back = (hidden_grad * up_proj * sigmoid_gate * (1.0 + gate_pre * (1.0 - sigmoid_gate))).astype(jnp.bfloat16)
        up_back = (hidden_grad * gate_pre * sigmoid_gate).astype(jnp.bfloat16)
        part = jnp.dot(gate_back, gate_mat, preferred_element_type=jnp.float32)
        part = part + jnp.dot(up_back, up_mat, preferred_element_type=jnp.float32)
        part_grad = lax.optimization_barrier(part.astype(jnp.bfloat16))
        summed = jnp.where(is_live[:, None], part_grad.astype(jnp.float32), jnp.zeros((), jnp.float32))
        running = running.at[safe_index].add(summed)
        down_grad = replica_sum(hidden, cot_rows, replicas)
        return running, down_grad

    start_grad = jnp.zeros(tokens.shape, jnp.float32)
    total_grad, grads = lax.scan(one_expert, start_grad, (token_table, prob_table, w_gate, w_up, w_down))
    weight_grad = jnp.transpose(grads, (1, 0, 2))
    return total_grad.astype(jnp.bfloat16), weight_grad
```

```python
import functools

import jax
import jax.numpy as jnp
from jax import lax
from jax.experimental import pallas as pl
from jax.experimental.pallas import tpu as pltpu
from jax.sharding import PartitionSpec as P

MESH = pl.DeviceIdType.MESH
F32 = jnp.float32
BF16 = jnp.bfloat16


def activate(gate_pre, up_proj, hidden_grad):
    sigmoid_gate = jax.nn.sigmoid(gate_pre)
    hidden = (gate_pre * sigmoid_gate * up_proj).astype(jnp.bfloat16)
    gate_back = (
        hidden_grad * up_proj * sigmoid_gate * (1.0 + gate_pre * (1.0 - sigmoid_gate))
    ).astype(jnp.bfloat16)
    up_back = (hidden_grad * gate_pre * sigmoid_gate).astype(jnp.bfloat16)
    return (hidden, gate_back, up_back)


def plain_on_device(tokens, cotangent, expert_ids, route_prob, popularity, w_gate, w_up, w_down):
    tok_rows = tokens.shape[0]
    model_width = tokens.shape[1]
    top_count = expert_ids.shape[1]
    expert_count = popularity.shape[0]
    local_count = w_gate.shape[0]
    pair_count = tok_rows * top_count
    capacity = pair_count // expert_count + max(1, pair_count // (4 * expert_count))
    owners = lax.axis_size("expert")
    replicas = lax.axis_size("dp") * lax.axis_size("outer")
    slot_total = expert_count * capacity
    onehot = (expert_ids[:, :, None] == popularity[None, None, :]).astype(jnp.int32)
    onehot = onehot.reshape(pair_count, expert_count)
    earlier = jnp.tril(jnp.ones((pair_count, pair_count), F32), -1)
    before = jnp.dot(earlier, onehot.astype(F32), precision="highest").astype(jnp.int32)
    place_rank = jnp.sum(onehot * before, axis=1)
    slot_index = jnp.sum(onehot * jnp.arange(expert_count, dtype=jnp.int32)[None, :], axis=1)
    target = slot_index * capacity + place_rank
    token_of = jnp.arange(pair_count, dtype=jnp.int32) // top_count
    slot_table = jnp.full((slot_total,), -1, jnp.int32).at[target].set(token_of)
    prob_table = jnp.zeros((slot_total,), jnp.float32).at[target].set(route_prob.reshape(-1))
    is_live = slot_table >= 0
    safe_index = jnp.maximum(slot_table, 0)
    send_rows = jnp.where(is_live[:, None], tokens[safe_index], jnp.zeros((), tokens.dtype))
    send_cot = (prob_table[:, None] * cotangent[safe_index].astype(jnp.float32)).astype(
        jnp.bfloat16
    )
    send_rows = send_rows.reshape(owners, local_count * capacity, model_width)
    send_cot = send_cot.reshape(owners, local_count * capacity, model_width)
    got_rows, got_cot = (
        lax.all_to_all(send_rows, "expert", split_axis=0, concat_axis=0, tiled=True),
        lax.all_to_all(send_cot, "expert", split_axis=0, concat_axis=0, tiled=True),
    )
    rows_four = got_rows.reshape(owners, local_count, capacity, model_width)
    gate_pre = jnp.einsum("slcd,lfd->slcf", rows_four, w_gate, preferred_element_type=jnp.float32)
    up_proj = jnp.einsum("slcd,lfd->slcf", rows_four, w_up, preferred_element_type=jnp.float32)
    cot_four = got_cot.reshape(owners, local_count, capacity, model_width)
    hidden_grad = jnp.einsum("slcd,lfd->slcf", cot_four, w_down, preferred_element_type=jnp.float32)
    hidden, gate_back, up_back = activate(gate_pre, up_proj, hidden_grad)
    back_rows = jnp.einsum("slcf,lfd->slcd", gate_back, w_gate, preferred_element_type=jnp.float32)
    back_rows = back_rows + jnp.einsum(
        "slcf,lfd->slcd", up_back, w_up, preferred_element_type=jnp.float32
    )
    back_rows = back_rows.astype(jnp.bfloat16).reshape(owners, local_count * capacity, model_width)
    came_back = lax.all_to_all(back_rows, "expert", split_axis=0, concat_axis=0, tiled=True)
    came_back = came_back.reshape(slot_total, model_width).astype(jnp.float32)
    came_back = jnp.where(is_live[:, None], came_back, jnp.zeros((), jnp.float32))
    token_grad = (
        jnp.zeros((tok_rows, model_width), jnp.float32)
        .at[safe_index]
        .add(came_back)
        .astype(jnp.bfloat16)
    )
    summed = lax.psum_scatter(
        jnp.einsum("slcf,slcd->fld", hidden, cot_four, preferred_element_type=jnp.float32).astype(
            jnp.bfloat16
        ),
        ("dp", "outer"),
        scatter_dimension=0,
        tiled=True,
    ).astype(jnp.float32)
    weight_grad = summed * (1.0 / replicas)
    return (token_grad, weight_grad)


def dot_nt(a, b):
    return lax.dot_general(a, b, (((1,), (1,)), ((), ())), preferred_element_type=F32)


def dot_nn(a, b):
    return lax.dot_general(a, b, (((1,), (0,)), ((), ())), preferred_element_type=F32)


def dot_tn(a, b):
    return lax.dot_general(a, b, (((0,), (0,)), ((), ())), preferred_element_type=F32)


def moe_kernel(
    owners, dps, outers, capacity,
    tok_hbm, cot_hbm, ids_hbm, prob_hbm, pop_hbm, wg_hbm, wu_hbm, wd_hbm,
    token_grad, weight_grad,
    tok, cot, ids, prob, pop, wg, wu, wd, tot, before, probs, send_x, recv_x, send_r, recv_r,
    cot_all, hid_all, dw, core_got, chip_send, chip_got,
    w_sem, xs_sem, xr_sem, rs_sem, rr_sem, cs_sem, cr_sem, ds_sem, dr_sem,
):
    me = lax.axis_index("expert")
    my_dp = lax.axis_index("dp")
    my_outer = lax.axis_index("outer")
    replicas = dps * outers
    half = owners // 2
    base = (me // half) * half
    other = half - base
    local = me - base
    tok_rows = tok.shape[0]

    loads = []
    for i, (src, dst) in enumerate((
        (ids_hbm, ids), (prob_hbm, prob), (pop_hbm, pop), (tok_hbm, tok), (cot_hbm, cot),
        (wg_hbm.at[0], wg), (wu_hbm.at[0], wu), (wd_hbm.at[0], wd),
    )):
        copy = pltpu.make_async_copy(src, dst, w_sem.at[i])
        copy.start()
        loads.append(copy)

    barrier = pltpu.get_barrier_semaphore()
    for k in range(1, owners):
        pl.semaphore_signal(
            barrier, inc=1, device_id={"expert": (me + k) % owners}, device_id_type=MESH
        )
    for i in range(1, dps):
        pl.semaphore_signal(
            barrier, inc=1, device_id={"dp": (my_dp + i) % dps}, device_id_type=MESH
        )
    for j in range(1, outers):
        pl.semaphore_signal(
            barrier, inc=1, device_id={"outer": (my_outer + j) % outers}, device_id_type=MESH
        )

    experts = pop.shape[1]
    for copy in loads[:3]:
        copy.wait()
    diagonal = lax.broadcasted_iota(jnp.int32, (experts, experts), 0) == lax.broadcasted_iota(
        jnp.int32, (experts, experts), 1
    )
    popv = jnp.sum(
        jnp.where(diagonal, pop[...].astype(F32), 0.0), axis=1, keepdims=True
    ).astype(jnp.int32)
    o0 = jnp.where(ids[0:1, :] == popv, 1.0, 0.0).astype(F32)
    o1 = jnp.where(ids[1:2, :] == popv, 1.0, 0.0).astype(F32)
    both = o0 + o1
    tot[...] = both
    probs[...] = o0 * prob[0:1, :] + o1 * prob[1:2, :]
    upper = lax.broadcasted_iota(jnp.int32, (tok_rows, tok_rows), 0) < lax.broadcasted_iota(
        jnp.int32, (tok_rows, tok_rows), 1
    )
    before[...] = dot_nn(both.astype(BF16), jnp.where(upper, 1.0, 0.0).astype(BF16))

    def select(slot):
        rank = lax.broadcasted_iota(jnp.int32, (capacity, tok_rows), 0).astype(F32)
        hit = jnp.where(rank == before[pl.ds(slot, 1), :], 1.0, 0.0).astype(F32)
        return hit * tot[pl.ds(slot, 1), :]

    def rows_for(slot):
        chosen = select(slot)
        weight = jnp.sum(chosen * probs[pl.ds(slot, 1), :], axis=1, keepdims=True)
        chosen = chosen.astype(BF16)
        return (
            dot_nn(chosen, tok[...]).astype(BF16),
            (weight * dot_nn(chosen, cot[...])).astype(BF16),
        )

    def x_copy(peer, at, sem_at):
        return pltpu.make_async_remote_copy(
            src_ref=send_x.at[peer],
            dst_ref=recv_x.at[at],
            send_sem=xs_sem.at[peer],
            recv_sem=xr_sem.at[sem_at],
            device_id={"expert": peer},
            device_id_type=MESH,
        )

    def r_copy(peer, at, sem_at):
        return pltpu.make_async_remote_copy(
            src_ref=send_r.at[peer],
            dst_ref=recv_r.at[at],
            send_sem=rs_sem.at[peer],
            recv_sem=rr_sem.at[sem_at],
            device_id={"expert": peer},
            device_id_type=MESH,
        )

    steps = [(i, j) for i in range(half // 2) for j in range(2)]

    def partner(start, i, j):
        return start + (local // 2 + i) % (half // 2) * 2 + (local + j) % 2

    far_to = [partner(other, i, j) for i, j in steps[::-1]]
    near_to = [partner(base, i, j) for i, j in steps[1:]]
    far_from = [partner(other, half // 2 - i, j) for i, j in steps[::-1]]
    near_from = [partner(base, half // 2 - i, j) for i, j in steps[1:]]

    loads[3].wait()
    loads[4].wait()
    waited = False
    early = far_to[: half // 2]
    late = far_to[half // 2 :]
    for place, peer in enumerate(early + near_to + late):
        rows, cots = rows_for(peer)
        send_x[peer, 0] = rows
        send_x[peer, 1] = cots
        if not waited:
            pl.semaphore_wait(barrier, owners + dps + outers - 3)
            waited = True
        if place < half - 1 + half // 2:
            x_copy(peer, me, me).start()
    rows, cots = rows_for(me)
    recv_x[me, 0] = rows
    recv_x[me, 1] = cots
    for done, peer in zip(early, late):
        x_copy(done, me, me).wait_send()
        x_copy(peer, me, me).start()
    for copy in loads[5:]:
        copy.wait()

    def process(sources, offset, between=None):
        for src, remote in sources:
            if remote:
                x_copy(src, src, src).wait_recv()
        x = jnp.concatenate([recv_x[s, 0].astype(F32) for s, _ in sources], axis=0).astype(BF16)
        c = jnp.concatenate([recv_x[s, 1].astype(F32) for s, _ in sources], axis=0).astype(BF16)
        count = len(sources) * capacity
        cot_all[pl.ds(offset, count), :] = c
        hidden, gate_back, up_back = activate(
            dot_nt(x, wg[...]), dot_nt(x, wu[...]), dot_nt(c, wd[...])
        )
        hid_all[pl.ds(offset, count), :] = hidden
        if between is not None:
            between()
        back = dot_nn(gate_back, wg[...]) + dot_nn(up_back, wu[...])
        for i, (src, remote) in enumerate(sources):
            rows = back[i * capacity : (i + 1) * capacity].astype(BF16)
            if remote:
                send_r[src] = rows
                r_copy(src, me, me).start()
            else:
                recv_r[src] = rows

    block = dw.shape[0] // replicas

    def block_at(rd, ro):
        return pl.ds(pl.multiple_of((rd * outers + ro) * block, 16), block)

    def core_copy(i, j):
        rd, ro = (my_dp + i) % dps, (my_outer + j) % outers
        at = (j - 1) * dps + i
        return pltpu.make_async_remote_copy(
            src_ref=dw.at[block_at(rd, ro), :],
            dst_ref=core_got.at[at],
            send_sem=cs_sem.at[at],
            recv_sem=cr_sem.at[at],
            device_id={"outer": ro},
            device_id_type=MESH,
        )

    def chip_copy(i):
        return pltpu.make_async_remote_copy(
            src_ref=chip_send.at[i - 1],
            dst_ref=chip_got.at[i - 1],
            send_sem=ds_sem.at[i - 1],
            recv_sem=dr_sem.at[i - 1],
            device_id={"dp": (my_dp + i) % dps},
            device_id_type=MESH,
        )

    chip_order = list(range(1, dps)) + [0]

    def start_gradient():
        dw[...] = dot_tn(hid_all[...], cot_all[...]).astype(BF16)
        for i in chip_order:
            for j in range(1, outers):
                core_copy(i, j).start()

    def chip_sum(i):
        total = dw[block_at((my_dp + i) % dps, my_outer), :].astype(F32)
        for j in range(1, outers):
            core_copy(i, j).wait_recv()
            total = total + core_got[(j - 1) * dps + i].astype(F32)
        return total

    near = [(me, False)] + [(s, True) for s in near_from]
    far = [(s, True) for s in far_from]
    process(near, 0)
    step = half
    for i in range(0, half, step):
        process(
            far[i : i + step],
            (half + i) * capacity,
            start_gradient if i + step >= half else None,
        )
    for i in range(1, dps):
        chip_send[i - 1] = chip_sum(i).astype(BF16)
        chip_copy(i).start()

    def combine(sources):
        for src, remote in sources:
            if remote:
                r_copy(src, src, src).wait_recv()
        chosen = jnp.concatenate([select(s) for s, _ in sources], axis=0).astype(BF16)
        rows = jnp.concatenate([recv_r[s].astype(F32) for s, _ in sources], axis=0).astype(BF16)
        return dot_tn(chosen, rows)

    near = [(me, False)] + [(s, True) for s in near_to]
    far = [(s, True) for s in far_to]
    total = combine(near)

    own = chip_sum(0)
    for i in range(1, dps):
        chip_copy(i).wait_recv()
        own = own + chip_got[i - 1].astype(F32)
    own = own * (1.0 / replicas)
    lanes = weight_grad.shape[1]
    parts = own.shape[1] // lanes
    for i in range(parts):
        weight_grad[pl.ds(i, block, stride=parts), :] = own[:, i * lanes : (i + 1) * lanes]

    token_grad[...] = (total + combine(far)).astype(BF16)

    for peer in near_to + late:
        x_copy(peer, me, me).wait_send()
    for peer in far_to + near_to:
        r_copy(peer, me, me).wait_send()
    for i in chip_order:
        for j in range(1, outers):
            core_copy(i, j).wait_send()
        if i:
            chip_copy(i).wait_send()


def on_device(tokens, cotangent, expert_ids, route_prob, popularity, w_gate, w_up, w_down):
    tok_rows, width = tokens.shape
    top_count = expert_ids.shape[1]
    experts = popularity.shape[0]
    local_count, hidden_units, _ = w_gate.shape
    owners = lax.axis_size("expert")
    dps, outers = lax.axis_size("dp"), lax.axis_size("outer")
    replicas = dps * outers
    pair_count = tok_rows * top_count
    capacity = pair_count // experts + max(1, pair_count // (4 * experts))
    block = hidden_units // replicas
    if local_count != 1 or top_count != 2 or capacity % 8 or block % 16 or owners % 4 or dps < 2 or outers < 2:
        return plain_on_device(
            tokens, cotangent, expert_ids, route_prob, popularity, w_gate, w_up, w_down
        )
    vmem = pl.BlockSpec(memory_space=pltpu.VMEM)
    hbm = pl.BlockSpec(memory_space=pltpu.HBM)
    weight = pltpu.VMEM((hidden_units, width), BF16)
    table = pltpu.VMEM((experts, tok_rows), F32)
    rows = owners * capacity
    token_grad, weight_grad = pl.pallas_call(
        functools.partial(moe_kernel, owners, dps, outers, capacity),
        out_shape=(
            jax.ShapeDtypeStruct((tok_rows, width), BF16),
            jax.ShapeDtypeStruct((block * width // 128, 128), F32),
        ),
        in_specs=[hbm] * 8,
        out_specs=(vmem, vmem),
        scratch_shapes=[
            pltpu.VMEM((tok_rows, width), BF16),
            pltpu.VMEM((tok_rows, width), BF16),
            pltpu.VMEM((top_count, tok_rows), jnp.int32),
            pltpu.VMEM((top_count, tok_rows), F32),
            pltpu.VMEM((1, experts), jnp.int32),
            weight, weight, weight, table, table, table,
            pltpu.VMEM((owners, 2, capacity, width), BF16),
            pltpu.VMEM((owners, 2, capacity, width), BF16),
            pltpu.VMEM((owners, capacity, width), BF16),
            pltpu.VMEM((owners, capacity, width), BF16),
            pltpu.VMEM((rows, width), BF16),
            pltpu.VMEM((rows, hidden_units), BF16),
            weight,
            pltpu.VMEM(((outers - 1) * dps, block, width), BF16),
            pltpu.VMEM((dps - 1, block, width), BF16),
            pltpu.VMEM((dps - 1, block, width), BF16),
            pltpu.SemaphoreType.DMA((8,)),
            pltpu.SemaphoreType.DMA((owners,)),
            pltpu.SemaphoreType.DMA((owners,)),
            pltpu.SemaphoreType.DMA((owners,)),
            pltpu.SemaphoreType.DMA((owners,)),
            pltpu.SemaphoreType.DMA(((outers - 1) * dps,)),
            pltpu.SemaphoreType.DMA(((outers - 1) * dps,)),
            pltpu.SemaphoreType.DMA((dps - 1,)),
            pltpu.SemaphoreType.DMA((dps - 1,)),
        ],
        compiler_params=pltpu.CompilerParams(
            collective_id=0, has_side_effects=True, vmem_limit_bytes=48 << 20
        ),
    )(
        *(
            pltpu.with_memory_space_constraint(array, pltpu.HBM)
            for array in (
                tokens, cotangent, expert_ids.T, route_prob.T,
                popularity.reshape(1, experts), w_gate, w_up, w_down,
            )
        )
    )
    return token_grad, weight_grad.reshape(block, 1, width)


def solution(mesh):
    placed = (
        P(("expert", "dp", "outer"), None),
        P(("expert", "dp", "outer"), None),
        P(("expert", "dp", "outer"), None),
        P(("expert", "dp", "outer"), None),
        P(),
        P("expert", None, None),
        P("expert", None, None),
        P("expert", None, None),
    )
    return jax.shard_map(
        on_device,
        mesh=mesh,
        in_specs=placed,
        out_specs=(P(("expert", "dp", "outer"), None), P(("dp", "outer"), "expert", None)),
        check_vma=False,
    )
```

```python
import functools

import jax
import jax.numpy as jnp
from jax import lax
from jax.experimental import pallas as pl
from jax.experimental.pallas import tpu as pltpu
from jax.sharding import PartitionSpec as P

MESH = pl.DeviceIdType.MESH
F32 = jnp.float32
BF16 = jnp.bfloat16


def activate(gate_pre, up_proj, hidden_grad):
    sigmoid_gate = jax.nn.sigmoid(gate_pre)
    hidden = (gate_pre * sigmoid_gate * up_proj).astype(jnp.bfloat16)
    gate_back = (
        hidden_grad * up_proj * sigmoid_gate * (1.0 + gate_pre * (1.0 - sigmoid_gate))
    ).astype(jnp.bfloat16)
    up_back = (hidden_grad * gate_pre * sigmoid_gate).astype(jnp.bfloat16)
    return (hidden, gate_back, up_back)


def plain_on_device(tokens, cotangent, expert_ids, route_prob, popularity, w_gate, w_up, w_down):
    tok_rows = tokens.shape[0]
    model_width = tokens.shape[1]
    top_count = expert_ids.shape[1]
    expert_count = popularity.shape[0]
    local_count = w_gate.shape[0]
    pair_count = tok_rows * top_count
    capacity = pair_count // expert_count + max(1, pair_count // (4 * expert_count))
    owners = lax.axis_size("expert")
    replicas = lax.axis_size("dp") * lax.axis_size("outer")
    slot_total = expert_count * capacity
    onehot = (expert_ids[:, :, None] == popularity[None, None, :]).astype(jnp.int32)
    onehot = onehot.reshape(pair_count, expert_count)
    earlier = jnp.tril(jnp.ones((pair_count, pair_count), F32), -1)
    before = jnp.dot(earlier, onehot.astype(F32), precision="highest").astype(jnp.int32)
    place_rank = jnp.sum(onehot * before, axis=1)
    slot_index = jnp.sum(onehot * jnp.arange(expert_count, dtype=jnp.int32)[None, :], axis=1)
    target = slot_index * capacity + place_rank
    token_of = jnp.arange(pair_count, dtype=jnp.int32) // top_count
    slot_table = jnp.full((slot_total,), -1, jnp.int32).at[target].set(token_of)
    prob_table = jnp.zeros((slot_total,), jnp.float32).at[target].set(route_prob.reshape(-1))
    is_live = slot_table >= 0
    safe_index = jnp.maximum(slot_table, 0)
    send_rows = jnp.where(is_live[:, None], tokens[safe_index], jnp.zeros((), tokens.dtype))
    send_cot = (prob_table[:, None] * cotangent[safe_index].astype(jnp.float32)).astype(
        jnp.bfloat16
    )
    send_rows = send_rows.reshape(owners, local_count * capacity, model_width)
    send_cot = send_cot.reshape(owners, local_count * capacity, model_width)
    got_rows, got_cot = (
        lax.all_to_all(send_rows, "expert", split_axis=0, concat_axis=0, tiled=True),
        lax.all_to_all(send_cot, "expert", split_axis=0, concat_axis=0, tiled=True),
    )
    rows_four = got_rows.reshape(owners, local_count, capacity, model_width)
    gate_pre = jnp.einsum("slcd,lfd->slcf", rows_four, w_gate, preferred_element_type=jnp.float32)
    up_proj = jnp.einsum("slcd,lfd->slcf", rows_four, w_up, preferred_element_type=jnp.float32)
    cot_four = got_cot.reshape(owners, local_count, capacity, model_width)
    hidden_grad = jnp.einsum("slcd,lfd->slcf", cot_four, w_down, preferred_element_type=jnp.float32)
    hidden, gate_back, up_back = activate(gate_pre, up_proj, hidden_grad)
    back_rows = jnp.einsum("slcf,lfd->slcd", gate_back, w_gate, preferred_element_type=jnp.float32)
    back_rows = back_rows + jnp.einsum(
        "slcf,lfd->slcd", up_back, w_up, preferred_element_type=jnp.float32
    )
    back_rows = back_rows.astype(jnp.bfloat16).reshape(owners, local_count * capacity, model_width)
    came_back = lax.all_to_all(back_rows, "expert", split_axis=0, concat_axis=0, tiled=True)
    came_back = came_back.reshape(slot_total, model_width).astype(jnp.float32)
    came_back = jnp.where(is_live[:, None], came_back, jnp.zeros((), jnp.float32))
    token_grad = (
        jnp.zeros((tok_rows, model_width), jnp.float32)
        .at[safe_index]
        .add(came_back)
        .astype(jnp.bfloat16)
    )
    summed = lax.psum_scatter(
        jnp.einsum("slcf,slcd->fld", hidden, cot_four, preferred_element_type=jnp.float32).astype(
            jnp.bfloat16
        ),
        ("dp", "outer"),
        scatter_dimension=0,
        tiled=True,
    ).astype(jnp.float32)
    weight_grad = summed * (1.0 / replicas)
    return (token_grad, weight_grad)


def dot_nt(a, b):
    return lax.dot_general(a, b, (((1,), (1,)), ((), ())), preferred_element_type=F32)


def dot_nn(a, b):
    return lax.dot_general(a, b, (((1,), (0,)), ((), ())), preferred_element_type=F32)


def dot_tn(a, b):
    return lax.dot_general(a, b, (((0,), (0,)), ((), ())), preferred_element_type=F32)


C_PARTS = 4
ABSENT = -1000.0


def place(half, outer_chip, y):
    return ((1 - half) * (1 - outer_chip) + half * (2 + outer_chip)) * 2 + y


def moe_kernel(
    capacity,
    tok_hbm, cot_hbm, ids_hbm, prob_hbm, pop_hbm, wg_hbm, wu_hbm, wd_hbm,
    token_grad, weight_grad,
    tok, cot, ids, prob, pop, wg, wu, wd, table, relay_table, relay_x, relay_c,
    near_pick, far_pick, send_n, recv_n, send_b, recv_b, send_ax, recv_ax, send_ac, recv_ac,
    send_nr, recv_nr, ret_a, got_a, ret_b, got_b, part, far_part,
    hid_all, c_all, dw, core_got, chip_send, chip_got,
    w_sem, ready, raw_s, raw_r, n_s, n_r, b_s, b_r, ax_s, ax_r, ac_s, ac_r,
    nr_s, nr_r, ra_s, ra_r, rb_s, rb_r, pa_s, pa_r, cs_s, cs_r, ch_s, ch_r,
):
    me = lax.axis_index("expert")
    my_dp = lax.axis_index("dp")
    my_outer = lax.axis_index("outer")
    z, y = me // 2, me % 2
    half = z // 2
    beside = 1 - y
    p = (z + half + 1) % 2
    inner = p == 0
    local = p * 2 + y
    tok_rows, width = tok.shape
    experts = pop.shape[1]
    wide = width // C_PARTS
    pair, quad = 2 * capacity, 4 * capacity
    peers = [((p + a) % 2, (y + b) % 2) for a, b in ((1, 0), (1, 1), (0, 1))]
    far_peers = [(1, y), (1, 1 - y), (0, 1 - y), (0, y)]

    def remote(src, dst, send_sem, recv_sem, **where):
        return pltpu.make_async_remote_copy(
            src_ref=src, dst_ref=dst, send_sem=send_sem, recv_sem=recv_sem,
            device_id=where, device_id_type=MESH,
        )

    loads = []
    for i, (src, dst) in enumerate((
        (ids_hbm, ids), (prob_hbm, prob), (pop_hbm, pop), (tok_hbm, tok), (cot_hbm, cot),
        (wg_hbm.at[0], wg), (wu_hbm.at[0], wu), (wd_hbm.at[0], wd),
    )):
        copy = pltpu.make_async_copy(src, dst, w_sem.at[i])
        copy.start()
        loads.append(copy)

    barrier = pltpu.get_barrier_semaphore()

    def greet(**where):
        pl.semaphore_signal(barrier, inc=1, device_id=where, device_id_type=MESH)

    greet(expert=place(1 - half, 0, y))

    @pl.when(inner)
    def _():
        greet(expert=place(1 - half, 1, y))
        greet(expert=place(1 - half, 0, 1 - y))

    for pp, yy in peers:
        greet(expert=place(half, pp, yy))
    greet(dp=1 - my_dp)
    greet(outer=1 - my_outer)

    sent = []
    role = [None]

    def go(make, *at):
        make(*at).start()
        sent.append((role[0], make, at))

    def when_inner(body):
        @pl.when(inner)
        def _():
            role[0] = True
            body()
            role[0] = None

    def when_not_inner(body):
        @pl.when(jnp.logical_not(inner))
        def _():
            role[0] = False
            body()
            role[0] = None

    def finish():
        for wanted, wrap in ((None, None), (True, when_inner), (False, when_not_inner)):
            def waits():
                for kept, make, at in sent:
                    if kept is wanted:
                        make(*at).wait_send()

            if wrap is None:
                waits()
            else:
                wrap(waits)

    def table_copy():
        return remote(table, relay_table, raw_s.at[0], raw_r.at[0], expert=place(1 - half, 0, y))

    def raw_x():
        return remote(tok, relay_x, raw_s.at[1], raw_r.at[1], expert=place(1 - half, 0, y))

    def raw_c():
        return remote(cot, relay_c, raw_s.at[2], raw_r.at[2], expert=place(1 - half, 0, y))

    def near_copy(pp, yy, slot):
        i = pp * 2 + yy
        return remote(
            send_n.at[i], recv_n.at[slot], n_s.at[i], n_r.at[slot], expert=place(half, pp, yy)
        )

    def near_return(pp, yy, slot):
        i = pp * 2 + yy
        return remote(
            send_nr.at[i], recv_nr.at[slot], nr_s.at[i], nr_r.at[slot], expert=place(half, pp, yy)
        )

    def direct_copy(pp, yy, slot):
        i = pp * 2 + yy
        return remote(
            send_b.at[i], recv_b.at[slot], b_s.at[i], b_r.at[slot], expert=place(1 - half, pp, yy)
        )

    def direct_return(yy, slot):
        return remote(
            ret_b.at[yy], got_b.at[slot], rb_s.at[yy], rb_r.at[slot], expert=place(1 - half, 0, yy)
        )

    def relay_x_copy(pp, yy, column):
        i = pp * 2 + yy
        return remote(
            send_ax.at[i], recv_ax.at[column], ax_s.at[i], ax_r.at[column],
            expert=place(half, pp, yy),
        )

    def relay_c_copy(pp, yy, column):
        i = pp * 2 + yy
        return remote(
            send_ac.at[i], recv_ac.at[column], ac_s.at[i], ac_r.at[column],
            expert=place(half, pp, yy),
        )

    def relay_return(yy, slot):
        return remote(
            ret_a.at[yy], got_a.at[slot], ra_s.at[yy], ra_r.at[slot], expert=place(half, 0, yy)
        )

    def part_copy():
        return remote(part, far_part, pa_s.at[0], pa_r.at[0], expert=place(1 - half, 1, y))

    block = dw.shape[1] // 4

    def block_at(rd, ro):
        return pl.ds(pl.multiple_of((rd * 2 + ro) * block, 16), block)

    def core_copy(k, i):
        rd, ro = (my_dp + i) % 2, 1 - my_outer
        return remote(
            dw.at[k, block_at(rd, ro), :], core_got.at[k, i],
            cs_s.at[k * 2 + i], cs_r.at[k * 2 + i], outer=ro,
        )

    def chip_copy(k):
        return remote(
            chip_send.at[k], chip_got.at[k], ch_s.at[k], ch_r.at[k], dp=1 - my_dp
        )

    for copy in loads[:3]:
        copy.wait()
    diagonal = lax.broadcasted_iota(jnp.int32, (experts, experts), 0) == lax.broadcasted_iota(
        jnp.int32, (experts, experts), 1
    )
    popv = jnp.sum(
        jnp.where(diagonal, pop[...].astype(F32), 0.0), axis=1, keepdims=True
    ).astype(jnp.int32)
    o0 = jnp.where(ids[0:1, :] == popv, 1.0, 0.0).astype(F32)
    o1 = jnp.where(ids[1:2, :] == popv, 1.0, 0.0).astype(F32)
    both = o0 + o1
    upper = lax.broadcasted_iota(jnp.int32, (tok_rows, tok_rows), 0) < lax.broadcasted_iota(
        jnp.int32, (tok_rows, tok_rows), 1
    )
    before = dot_nn(both.astype(BF16), jnp.where(upper, 1.0, 0.0).astype(BF16))
    table[0:experts, :] = jnp.where(both > 0.0, before, ABSENT)
    table[experts : 2 * experts, :] = o0 * prob[0:1, :] + o1 * prob[1:2, :]

    def picks(source, chosen_half):
        rank = lax.broadcasted_iota(jnp.int32, (capacity, tok_rows), 0).astype(F32)
        hits, weights = [], []
        for s in range(4):
            e = place(chosen_half, s // 2, s % 2)
            hit = jnp.where(rank == source[pl.ds(e, 1), :], 1.0, 0.0).astype(F32)
            hits.append(hit)
            weights.append(
                jnp.sum(hit * source[pl.ds(experts + e, 1), :], axis=1, keepdims=True)
            )
        return jnp.concatenate(hits, axis=0).astype(BF16), jnp.concatenate(weights, axis=0)

    def slot_rows(value, s):
        return value[s * capacity : (s + 1) * capacity].astype(BF16)

    def stack(slots):
        return jnp.concatenate([slot.astype(F32) for slot in slots], axis=0).astype(BF16)

    def fill(to, chosen, weight):
        rows = dot_nn(chosen, tok[...])
        cots = weight * dot_nn(chosen, cot[...])
        for s in range(4):
            to[s, 0] = slot_rows(rows, s)
            to[s, 1] = slot_rows(cots, s)

    chosen, weight = picks(table, half)
    near_pick[...] = chosen
    loads[3].wait()
    loads[4].wait()
    fill(send_n, chosen, weight)

    @when_inner
    def _():
        chosen, weight = picks(table, 1 - half)
        far_pick[...] = chosen
        fill(send_b, chosen, weight)

    pl.semaphore_wait(barrier, 8 - 2 * p)

    @when_not_inner
    def _():
        go(table_copy)
        go(raw_x)
        go(raw_c)

    @when_inner
    def _():
        pl.semaphore_signal(
            ready, inc=1, device_id={"expert": place(1 - half, 0, y)}, device_id_type=MESH
        )

    for pp, yy in peers:
        go(near_copy, pp, yy, local)
    recv_n[local] = send_n[local]

    @when_inner
    def _():
        for pp, yy in far_peers[2:]:
            go(direct_copy, pp, yy, y)

    for copy in loads[5:]:
        copy.wait()

    def process(x, c, offset):
        count = x.shape[0]
        c_all[offset : offset + count, :] = c
        hidden, gate_back, up_back = activate(
            dot_nt(x, wg[...]), dot_nt(x, wu[...]), dot_nt(c, wd[...])
        )
        hid_all[offset : offset + count, :] = hidden
        return dot_nn(gate_back, wg[...]) + dot_nn(up_back, wu[...])

    def near_rows():
        for pp, yy in peers:
            near_copy(pp, yy, pp * 2 + yy).wait_recv()
        back = process(
            stack([recv_n[s, 0] for s in range(4)]), stack([recv_n[s, 1] for s in range(4)]), 0
        )
        for s in range(4):
            send_nr[s] = slot_rows(back, s)
        for pp, yy in peers:
            go(near_return, pp, yy, local)
        recv_nr[local] = send_nr[local]

    def relay_tokens():
        table_copy().wait_recv()
        chosen, weight = picks(relay_table, half)
        raw_x().wait_recv()
        rows = dot_nn(chosen, relay_x[...])
        for s in range(4):
            send_ax[s] = slot_rows(rows, s)
        for pp, yy in peers:
            go(relay_x_copy, pp, yy, y)
        recv_ax[y] = send_ax[local]
        raw_c().wait_recv()
        cots = weight * dot_nn(chosen, relay_c[...])
        for s in range(4):
            send_ac[s] = slot_rows(cots, s)
        for pp, yy in peers:
            go(relay_c_copy, pp, yy, y)
        pl.semaphore_wait(ready, 1)
        for pp, yy in far_peers[:2]:
            go(direct_copy, pp, yy, y)
        recv_ac[y] = send_ac[local]

    def relayed_rows(here):
        for copy in (relay_x_copy, relay_c_copy):
            copy(0, beside, beside).wait_recv()
            if not here:
                copy(0, y, y).wait_recv()
        back = process(
            stack([recv_ax[s] for s in range(2)]), stack([recv_ac[s] for s in range(2)]), quad
        )
        for s in range(2):
            ret_a[s] = slot_rows(back, s)
        go(relay_return, beside, local)
        if here:
            got_a[local] = ret_a[y]
        else:
            go(relay_return, y, local)

    def relay_sums():
        for pp, yy in peers:
            relay_return(y, pp * 2 + yy).wait_recv()
        chosen, _ = picks(relay_table, half)
        part[...] = dot_tn(chosen, stack([got_a[s] for s in range(4)])).astype(BF16)
        go(part_copy)

    def direct_rows():
        for s in range(2):
            direct_copy(0, s, s).wait_recv()
        back = process(
            stack([recv_b[s, 0] for s in range(2)]),
            stack([recv_b[s, 1] for s in range(2)]),
            quad + pair,
        )
        for s in range(2):
            ret_b[s] = slot_rows(back, s)
            go(direct_return, s, local)

    @when_not_inner
    def _():
        near_rows()
        relayed_rows(False)
        direct_rows()

    @when_inner
    def _():
        relay_tokens()
        relayed_rows(True)
        direct_rows()
        near_rows()
        relay_sums()

    def chip_sum(k, i):
        core_copy(k, i).wait_recv()
        rd = (my_dp + i) % 2
        return dw[k, block_at(rd, my_outer), :].astype(F32) + core_got[k, i].astype(F32)

    def to_chip(k):
        chip_send[k] = chip_sum(k, 1).astype(BF16)
        go(chip_copy, k)

    for k in range(C_PARTS):
        dw[k] = dot_tn(hid_all[...], c_all[:, k * wide : (k + 1) * wide]).astype(BF16)
        for i in (1, 0):
            go(core_copy, k, i)
        if k:
            to_chip(k - 1)
    to_chip(C_PARTS - 1)

    for pp, yy in peers:
        near_return(pp, yy, pp * 2 + yy).wait_recv()
    total = dot_tn(near_pick[...], stack([recv_nr[s] for s in range(4)]))

    lanes = weight_grad.shape[1]
    parts = width // lanes
    for k in range(C_PARTS):
        own = chip_sum(k, 0)
        chip_copy(k).wait_recv()
        own = (own + chip_got[k].astype(F32)) * 0.25
        for j in range(wide // lanes):
            weight_grad[pl.ds(k * (wide // lanes) + j, block, stride=parts), :] = own[
                :, j * lanes : (j + 1) * lanes
            ]

    @when_not_inner
    def _():
        part_copy().wait_recv()
        token_grad[...] = (total + far_part[...].astype(F32)).astype(BF16)

    @when_inner
    def _():
        for s in range(4):
            direct_return(0, s).wait_recv()
        far = dot_tn(far_pick[...], stack([got_b[s] for s in range(4)]))
        token_grad[...] = (total + far).astype(BF16)

    finish()


def on_device(tokens, cotangent, expert_ids, route_prob, popularity, w_gate, w_up, w_down):
    tok_rows, width = tokens.shape
    top_count = expert_ids.shape[1]
    experts = popularity.shape[0]
    local_count, hidden_units, _ = w_gate.shape
    owners = lax.axis_size("expert")
    dps, outers = lax.axis_size("dp"), lax.axis_size("outer")
    pair_count = tok_rows * top_count
    capacity = pair_count // experts + max(1, pair_count // (4 * experts))
    block = hidden_units // (dps * outers)
    if (
        local_count != 1 or top_count != 2 or capacity % 8 or block % 16 or tok_rows != 128
        or owners != 8 or dps != 2 or outers != 2 or width % 512
    ):
        return plain_on_device(
            tokens, cotangent, expert_ids, route_prob, popularity, w_gate, w_up, w_down
        )
    vmem = pl.BlockSpec(memory_space=pltpu.VMEM)
    hbm = pl.BlockSpec(memory_space=pltpu.HBM)
    weight = pltpu.VMEM((hidden_units, width), BF16)
    rows = pltpu.VMEM((tok_rows, width), BF16)
    wide = width // C_PARTS
    quad = 4 * capacity

    def dma(count):
        return pltpu.SemaphoreType.DMA((count,))

    def slots(*count):
        return pltpu.VMEM((*count, capacity, width), BF16)

    token_grad, weight_grad = pl.pallas_call(
        functools.partial(moe_kernel, capacity),
        out_shape=(
            jax.ShapeDtypeStruct((tok_rows, width), BF16),
            jax.ShapeDtypeStruct((block * width // 128, 128), F32),
        ),
        in_specs=[hbm] * 8,
        out_specs=(vmem, vmem),
        scratch_shapes=[
            rows, rows,
            pltpu.VMEM((top_count, tok_rows), jnp.int32),
            pltpu.VMEM((top_count, tok_rows), F32),
            pltpu.VMEM((1, experts), jnp.int32),
            weight, weight, weight,
            pltpu.VMEM((2 * experts, tok_rows), F32),
            pltpu.VMEM((2 * experts, tok_rows), F32),
            rows, rows,
            pltpu.VMEM((quad, tok_rows), BF16),
            pltpu.VMEM((quad, tok_rows), BF16),
            slots(4, 2), slots(4, 2), slots(4, 2), slots(2, 2),
            slots(4), slots(2), slots(4), slots(2),
            slots(4), slots(4), slots(2), slots(4), slots(2), slots(4),
            rows, rows,
            pltpu.VMEM((2 * quad, hidden_units), BF16),
            pltpu.VMEM((2 * quad, width), BF16),
            pltpu.VMEM((C_PARTS, hidden_units, wide), BF16),
            pltpu.VMEM((C_PARTS, 2, block, wide), BF16),
            pltpu.VMEM((C_PARTS, block, wide), BF16),
            pltpu.VMEM((C_PARTS, block, wide), BF16),
            dma(8),
            pltpu.SemaphoreType.REGULAR,
            dma(3), dma(3), dma(4), dma(4), dma(4), dma(2),
            dma(4), dma(2), dma(4), dma(2),
            dma(4), dma(4), dma(2), dma(4), dma(2), dma(4),
            dma(1), dma(1),
            dma(2 * C_PARTS), dma(2 * C_PARTS),
            dma(C_PARTS), dma(C_PARTS),
        ],
        compiler_params=pltpu.CompilerParams(
            collective_id=0, has_side_effects=True, vmem_limit_bytes=48 << 20
        ),
    )(
        *(
            pltpu.with_memory_space_constraint(array, pltpu.HBM)
            for array in (
                tokens, cotangent, expert_ids.T, route_prob.T,
                popularity.reshape(1, experts), w_gate, w_up, w_down,
            )
        )
    )
    return token_grad, weight_grad.reshape(block, 1, width)


def solution(mesh):
    placed = (
        P(("expert", "dp", "outer"), None),
        P(("expert", "dp", "outer"), None),
        P(("expert", "dp", "outer"), None),
        P(("expert", "dp", "outer"), None),
        P(),
        P("expert", None, None),
        P("expert", None, None),
        P("expert", None, None),
    )
    return jax.shard_map(
        on_device,
        mesh=mesh,
        in_specs=placed,
        out_specs=(P(("expert", "dp", "outer"), None), P(("dp", "outer"), "expert", None)),
        check_vma=False,
    )
```
